128 devices in a mesh: row: 8 (over x_hi, y), col: 16 (over x_lo, z, core).
Axes of the slice: x: 4 (x_hi: 2, x_lo: 2; x = x_hi * 2 + x_lo), y: 4, z: 4, core: 2. Of those that a mesh axis runs over, the one named last changes fastest.
Arguments:
- tile_values: bfloat16 [49152, 128, 128], P(('row', 'col')), as said below
- tile_coords: int32 [49152, 2], P(('row', 'col')), may hold values from 0 to 63, as said below
- tile_count: int32 [128], P(('row', 'col')), may hold values from 48 to 384, as said below
- hub_prior: bfloat16 [65536, 128], P(('row', 'col')), may hold values from -6 to 6
- out_degree: int32 [65536], P('row'), may hold values from 1 to 8
- in_degree: int32 [65536], P('col'), may hold values from 1 to 8
- seed_ids: int32 [128], replicated, may hold values from 0 to 65535
Outputs:
- hub_scores: float32 [65536, 128], P(('row', 'col'))
- authority_scores: float32 [65536, 128], P(('col', 'row'))
The draws below stay inside these ranges and needn't reach their ends.
Inputs may be any that keep to these rules, and one draw needn't show every extreme that they name: `tile_count`: every device has at least 48 live slots, and in every draw all devices of some column group have exactly 384. `tile_coords`: entry 0 lies below 64, entry 1 below 32; no two slots of one device name the same pair. Slots that are not live hold pairs too. `tile_values`: entries are zero where no follow edge exists.
All inputs are finite; a program needn't handle non-finite values.
Results may differ from the reference program's by a relative error of at most 0.0034.
The reference program's roundings to bfloat16 on the way count: a program that leaves them out, or rounds other values in their place, can miss the bound.
Values may be sent and summed in bfloat16 or wider, within the bound.
No kernel may reach another device: no remote copies, remote signals or barrier semaphores. Data moves between devices by JAX's collectives and lax.ppermute only.
A program may use at most 128 MiB of HBM per device.

```python
import jax
import jax.numpy as jnp
from jax import lax

TB = 128
S = 128
UB = 4
CAP = 384
SWEEPS = 2
FBR = 64
FBC = 32
USERS = 65536
TILES = 49152
N_ROW = 8
N_COL = 16
DEVICES = 128


def draw_tile_count(key, part):
    key_full, key_light = jax.random.split(jax.random.fold_in(key, 11))
    full_group = jax.random.randint(key_full, (), 0, N_COL)
    light = jax.random.randint(key_light, (DEVICES,), CAP // 8, CAP // 3 + 1)
    groups = jnp.arange(DEVICES) % N_COL
    return jnp.where(groups == full_group, CAP, light).astype(jnp.int32)


def pick_slots(device_key):
    return jax.random.permutation(device_key, FBR * FBC)[:CAP]


def draw_tile_coords(key, part):
    device_keys = jax.random.split(jax.random.fold_in(key, 23), DEVICES)
    picks = jax.vmap(pick_slots)(device_keys)
    coords = jnp.stack([picks // FBC, picks % FBC], axis=-1)
    return coords.reshape(TILES, 2).astype(jnp.int32)


def draw_tile_values(key, part):
    key_edge, key_value = jax.random.split(jax.random.fold_in(key, 37), 2)
    shape = (TILES, TB, TB)
    edges = (jax.random.uniform(key_edge, shape) < 0.5).astype(jnp.float32)
    values = jax.random.normal(key_value, shape, jnp.float32)
    return (edges * values * (4.0 * TB) ** (-0.5)).astype(jnp.bfloat16)


def plant(entries, rng, smallest, largest):
    extent = entries.shape
    index_at = [jax.random.randint(jax.random.fold_in(rng, axis), (), 0, extent[axis]) for axis in range(len(extent))]
    entries = entries.at[tuple(index_at)].set(smallest)
    longest = extent.index(max(extent))
    index_at[longest] = (index_at[longest] + 1) % extent[longest]
    return entries.at[tuple(index_at)].set(largest)


def block_levels(key, dims, shards, low, largest):
    level, own = 1.0, jax.random.fold_in(key, 6)
    for position, blocks in shards:
        draws = jnp.exp(jax.random.uniform(jax.random.fold_in(own, position), (blocks,), jnp.float32, low / len(shards), largest / len(shards)))
        level = level * jnp.repeat(draws, dims[position] // blocks).reshape([-1 if axis == position else 1 for axis in range(len(dims))])
    return level


def bell_draw(key, extent, scale, most, cuts=(), held_as=jnp.bfloat16):
    gain = block_levels(key, extent, cuts, -0.22, 0.18) if cuts else 1.0
    array = jax.random.normal(key, extent, jnp.float32) * scale * gain
    return jnp.minimum(jnp.maximum(array, -most), most).astype(held_as)


def setup_inputs(seed: int = 0) -> dict:
    streams_of = jax.random.split(jax.random.key(seed), 8)
    return {
        "tile_values": draw_tile_values(jax.random.fold_in(streams_of[7], 71), 0),
        "tile_coords": draw_tile_coords(jax.random.fold_in(streams_of[7], 71), 0),
        "tile_count": draw_tile_count(jax.random.fold_in(streams_of[7], 71), 0),
        "hub_prior": bell_draw(streams_of[3], (USERS, S), 1.0, 6.0, ((0, 128),)),
        "out_degree": plant(jax.random.randint(streams_of[4], (USERS,), 1, 9), jax.random.fold_in(streams_of[4], 1), 1, 8).astype(jnp.int32),
        "in_degree": plant(jax.random.randint(streams_of[5], (USERS,), 1, 9), jax.random.fold_in(streams_of[5], 1), 1, 8).astype(jnp.int32),
        "seed_ids": plant(jax.random.randint(streams_of[6], (S,), 0, USERS), jax.random.fold_in(streams_of[6], 1), 0, USERS - 1).astype(jnp.int32),
    }


reset_share = 0.3


def reference(tile_values, tile_coords, tile_count, hub_prior, out_degree, in_degree, seed_ids):
    follower_blocks = UB * N_COL
    followee_blocks = UB * N_ROW
    user_blocks = USERS // TB
    values_dev = tile_values.reshape(DEVICES, CAP, TB, TB)
    coords_dev = tile_coords.reshape(DEVICES, CAP, 2)
    devices = jnp.arange(DEVICES, dtype=jnp.int32)
    row_group = devices // N_COL
    col_group = devices % N_COL
    follower_ids = (row_group[:, None] * follower_blocks + coords_dev[:, :, 0]).astype(jnp.int32)
    followee_ids = (col_group[:, None] * followee_blocks + coords_dev[:, :, 1]).astype(jnp.int32)
    live = (jnp.arange(CAP, dtype=jnp.int32)[None, :] < tile_count[:, None]).astype(jnp.float32)

    def to_authority(spread):
        panel = spread.reshape(user_blocks, TB, S)

        def one_device(total, device):
            block = values_dev[device].astype(jnp.float32)
            picked = panel[follower_ids[device]].astype(jnp.float32)
            product = jnp.einsum("kij,kis->kjs", block, picked, precision=lax.Precision.HIGHEST)
            product = product * live[device][:, None, None]
            return total.at[followee_ids[device]].add(product), None

        total, _ = lax.scan(one_device, jnp.zeros((user_blocks, TB, S), jnp.float32), devices)
        return total.reshape(USERS, S)

    def to_hub(lent):
        panel = lent.reshape(user_blocks, TB, S)

        def one_device(total, device):
            block = values_dev[device].astype(jnp.float32)
            picked = panel[followee_ids[device]].astype(jnp.float32)
            product = jnp.einsum("kij,kjs->kis", block, picked, precision=lax.Precision.HIGHEST)
            product = product * live[device][:, None, None]
            return total.at[follower_ids[device]].add(product), None

        total, _ = lax.scan(one_device, jnp.zeros((user_blocks, TB, S), jnp.float32), devices)
        return total.reshape(USERS, S)

    users = jnp.arange(USERS, dtype=jnp.int32)
    seed_hit = (users[:, None] == seed_ids[None, :]).astype(jnp.float32)
    hub = hub_prior.astype(jnp.float32)
    authority = jnp.zeros((USERS, S), jnp.float32)
    for sweep_number in range(SWEEPS):
        spread = (hub / out_degree.astype(jnp.float32)[:, None]).astype(jnp.bfloat16)
        authority = to_authority(spread) / in_degree.astype(jnp.float32)[:, None]
        lent = authority.astype(jnp.bfloat16)
        hub = (1.0 - reset_share) * to_hub(lent) + reset_share * seed_hit
    return hub, authority
```

```python
import functools

import jax
import jax.numpy as jnp
from jax import lax
from jax.experimental import pallas as pl
from jax.experimental.pallas import tpu as pltpu
from jax.sharding import PartitionSpec as P

SWEEPS = 2
RESET = 0.3
SIDE = 128
Y = 4
Z = 4
CHUNK = 32
UNROLL = 8
TAG = 16
TOP = 14


def products_kernel(
    own_blocks, pieces, targets, forward, live_ref, order_ref, from_ref, to_ref, *refs
):
    piece_refs = refs[:pieces]
    tiles_hbm = refs[pieces]
    out_ref = refs[pieces + 1]
    panel, tiles, total, tile_sem, piece_sem = refs[pieces + 2 :]
    cap = tiles.shape[0]
    blocks = targets * own_blocks
    live = live_ref[0]

    def tile_copy(number):
        rows = pl.ds(number * CHUNK, CHUNK)
        return pltpu.make_async_copy(tiles_hbm.at[rows], tiles.at[rows], tile_sem.at[number])

    def piece_copy(number):
        rows = pl.ds(order_ref[number] * own_blocks, own_blocks)
        return pltpu.make_async_copy(piece_refs[number], panel.at[rows], piece_sem.at[number])

    for number in range(pieces):
        piece_copy(number).start()
    for number in range(cap // CHUNK):

        @pl.when(number * CHUNK < live)
        def _():
            tile_copy(number).start()

    def clear(block, _):
        total[block] = jnp.zeros((SIDE, SIDE), jnp.float32)
        return 0

    lax.fori_loop(0, blocks, clear, 0)
    for number in range(pieces):
        piece_copy(number).wait()

    def group(first):
        parts = []
        for step in range(UNROLL):
            slot = first + step
            block = tiles[slot]
            picked = panel[from_ref[slot]]
            if forward:
                part = jnp.dot(picked, block, preferred_element_type=jnp.float32)
            else:
                part = jnp.dot(block, picked, preferred_element_type=jnp.float32)
            parts.append((jnp.where(slot < live, to_ref[slot], blocks), part))
        for target, part in parts:
            total[target] += part

    def chunk(number, _):
        tile_copy(number).wait()

        def step(inner, _):
            group(number * CHUNK + inner * UNROLL)
            return 0

        left = jnp.minimum(live - number * CHUNK, CHUNK)
        lax.fori_loop(0, pl.cdiv(left, UNROLL), step, 0)
        return 0

    lax.fori_loop(0, pl.cdiv(live, CHUNK), chunk, 0)

    def finish(target, _):
        for inner in range(own_blocks):
            part = total[target * own_blocks + inner]
            most = jnp.max(jnp.abs(part), axis=0, keepdims=True)
            power = jnp.floor(jnp.log2(jnp.maximum(most, 1e-30))) + 1.0
            coded = jnp.round(part * jnp.exp2(TOP - power))
            coded = jnp.clip(coded, -32767.0, 32767.0)
            out_ref[target, inner * SIDE : (inner + 1) * SIDE, :] = coded.astype(
                jnp.int32
            ).astype(jnp.int16)
            out_ref[target, own_blocks * SIDE + inner * TAG : own_blocks * SIDE + (inner + 1) * TAG, :] = (
                jnp.broadcast_to(power, (TAG, SIDE)).astype(jnp.int32).astype(jnp.int16)
            )
        return 0

    lax.fori_loop(0, targets, finish, 0)


def products(tile_values, pieces, order, from_block, to_block, live, targets, forward):
    own_blocks = pieces[0].shape[0]
    cap = tile_values.shape[0]
    count = len(pieces)
    rows = own_blocks * (SIDE + TAG)
    smem = pl.BlockSpec(memory_space=pltpu.SMEM)
    anywhere = pl.BlockSpec(memory_space=pl.ANY)
    return pl.pallas_call(
        functools.partial(products_kernel, own_blocks, count, targets, forward),
        out_shape=jax.ShapeDtypeStruct((targets, rows, SIDE), jnp.int16),
        in_specs=[smem] * 4 + [anywhere] * (count + 1),
        out_specs=pl.BlockSpec(memory_space=pltpu.VMEM),
        scratch_shapes=[
            pltpu.VMEM((count * own_blocks, SIDE, SIDE), jnp.bfloat16),
            pltpu.VMEM((cap, SIDE, SIDE), jnp.bfloat16),
            pltpu.VMEM((targets * own_blocks + 1, SIDE, SIDE), jnp.float32),
            pltpu.SemaphoreType.DMA((cap // CHUNK,)),
            pltpu.SemaphoreType.DMA((count,)),
        ],
        compiler_params=pltpu.CompilerParams(vmem_limit_bytes=40 << 20),
    )(live, order, from_block, to_block, *pieces, tile_values)


def combined(in_ref, inner, own_blocks):
    value = None
    for source in range(in_ref.shape[0]):
        coded = in_ref[source, inner * SIDE : (inner + 1) * SIDE, :]
        tag = own_blocks * SIDE + inner * TAG
        power = in_ref[source, tag : tag + TAG, :].astype(jnp.int32).astype(jnp.float32)[:1]
        part = coded.astype(jnp.int32).astype(jnp.float32) * jnp.exp2(power - TOP)
        value = part if value is None else value + part
    return value


def authority_kernel(in_ref, degree_ref, lent_ref, score_ref=None):
    own_blocks = lent_ref.shape[0]
    for inner in range(own_blocks):
        degree = degree_ref[inner : inner + 1, :].astype(jnp.float32)
        score = jnp.transpose(combined(in_ref, inner, own_blocks) / degree)
        lent_ref[inner] = score.astype(jnp.bfloat16)
        if score_ref is not None:
            score_ref[inner * SIDE : (inner + 1) * SIDE, :] = score


def hub_kernel(in_ref, seed_ref, first_ref, degree_ref, out_ref, last):
    own_blocks = degree_ref.shape[0]
    for inner in range(own_blocks):
        users = (
            first_ref[0]
            + inner * SIDE
            + lax.broadcasted_iota(jnp.int32, (SIDE, SIDE), 0)
        )
        hit = (users == seed_ref[...]).astype(jnp.float32)
        hub = (1.0 - RESET) * combined(in_ref, inner, own_blocks) + RESET * hit
        if last:
            out_ref[inner * SIDE : (inner + 1) * SIDE, :] = hub
        else:
            degree = degree_ref[inner : inner + 1, :].astype(jnp.float32)
            out_ref[inner] = (jnp.transpose(hub) / degree).astype(jnp.bfloat16)


def prior_kernel(hub_ref, degree_ref, out_ref):
    for inner in range(out_ref.shape[0]):
        hub = hub_ref[inner * SIDE : (inner + 1) * SIDE, :].astype(jnp.float32)
        degree = degree_ref[inner : inner + 1, :].astype(jnp.float32)
        out_ref[inner] = (jnp.transpose(hub) / degree).astype(jnp.bfloat16)


def per_device(tile_values, tile_coords, tile_count, hub_prior, out_degree, in_degree, seed_ids):
    row_size = lax.axis_size("row")
    col_size = lax.axis_size("col")
    row_index = lax.axis_index("row")
    col_index = lax.axis_index("col")
    slice_rows = hub_prior.shape[0]
    own_blocks = slice_rows // SIDE
    x_hi = row_size // Y
    x_lo = col_size // (2 * Z)

    own_out = lax.dynamic_slice_in_dim(out_degree, col_index * slice_rows, slice_rows)
    own_out = own_out.reshape(own_blocks, SIDE)
    own_in = lax.dynamic_slice_in_dim(in_degree, row_index * slice_rows, slice_rows)
    own_in = own_in.reshape(own_blocks, SIDE)
    first_user = ((row_index * col_size + col_index) * slice_rows).astype(jnp.int32)[None]
    seeds = seed_ids[None, :]
    follower = tile_coords[:, 0]
    followee = tile_coords[:, 1]

    def row_at(a, b):
        return (a % x_hi) * Y + b % Y

    def col_at(a, b, c):
        return ((a % x_lo) * Z + b % Z) * 2 + c % 2

    def gather_row(piece):
        pieces, order = [piece], [row_index]
        a, b = row_index // Y, row_index % Y
        for da in range(x_hi):
            for db in range(Y):
                if (da, db) == (0, 0):
                    continue
                links = [
                    (row_at(i, j), row_at(i + da, j + db)) for i in range(x_hi) for j in range(Y)
                ]
                pieces.append(lax.ppermute(piece, "row", links))
                order.append(row_at(a - da + x_hi, b - db + Y))
        return pieces, jnp.stack(order).astype(jnp.int32)

    def gather_col(piece):
        pieces, order = [piece], [col_index]
        a, b, c = col_index // (2 * Z), (col_index // 2) % Z, col_index % 2
        swap = [
            (col_at(i, j, k), col_at(i, j, k + 1))
            for i in range(x_lo)
            for j in range(Z)
            for k in range(2)
        ]
        for da in range(x_lo):
            for db in range(Z):
                if (da, db) == (0, 0):
                    continue
                links = [
                    (col_at(i, j, k), col_at(i + da, j + db, k))
                    for i in range(x_lo)
                    for j in range(Z)
                    for k in range(2)
                ]
                pieces.append(lax.ppermute(piece, "col", links))
                order.append(col_at(a - da + x_lo, b - db + Z, c))
        for number in range(len(pieces)):
            pieces.append(lax.ppermute(pieces[number], "col", swap))
            order.append(order[number] + 1 - 2 * c)
        return pieces, jnp.stack(order).astype(jnp.int32)

    spread = pl.pallas_call(
        prior_kernel,
        out_shape=jax.ShapeDtypeStruct((own_blocks, SIDE, SIDE), jnp.bfloat16),
    )(hub_prior, own_out)

    vmem = pl.BlockSpec(memory_space=pltpu.VMEM)
    smem = pl.BlockSpec(memory_space=pltpu.SMEM)
    authority_scores = hub_scores = None
    for sweep_number in range(SWEEPS):
        last = sweep_number + 1 == SWEEPS
        pieces, order = gather_col(spread)
        partial = products(
            tile_values, pieces, order, follower, followee, tile_count, row_size, True
        )
        mine = lax.all_to_all(partial, "row", 0, 0, tiled=True)
        lent_type = jax.ShapeDtypeStruct((own_blocks, SIDE, SIDE), jnp.bfloat16)
        score_type = jax.ShapeDtypeStruct((slice_rows, SIDE), jnp.float32)
        lent = pl.pallas_call(
            authority_kernel,
            out_shape=(lent_type, score_type) if last else (lent_type,),
        )(mine, own_in)
        if last:
            authority_scores = lent[1]
        pieces, order = gather_row(lent[0])
        partial = products(
            tile_values, pieces, order, followee, follower, tile_count, col_size, False
        )
        mine = lax.all_to_all(partial, "col", 0, 0, tiled=True)
        hub = pl.pallas_call(
            functools.partial(hub_kernel, last=last),
            out_shape=score_type if last else lent_type,
            in_specs=[vmem, vmem, smem, vmem],
            out_specs=vmem,
        )(mine, seeds, first_user, own_out)
        if last:
            hub_scores = hub
        else:
            spread = hub
    return (hub_scores, authority_scores)


def solution(mesh):
    placed = (
        P(("row", "col"), None, None),
        P(("row", "col"), None),
        P(("row", "col")),
        P(("row", "col"), None),
        P("row"),
        P("col"),
        P(),
    )
    return jax.shard_map(
        per_device,
        mesh=mesh,
        in_specs=placed,
        out_specs=(P(("row", "col"), None), P(("col", "row"), None)),
        check_vma=False,
    )
```

```python
import functools

import jax
import jax.numpy as jnp
from jax import lax
from jax.experimental import pallas as pl
from jax.experimental.pallas import tpu as pltpu
from jax.sharding import PartitionSpec as P

SWEEPS = 2
RESET = 0.3
SIDE = 128
CORES = 2
QUAD = 4
UNROLL = 6
BITS = 6
FIELD = 1 << BITS
SMALL = 8 << 20
LARGE = 24 << 20
TAG = 16
TOP = 15
MARGIN = 0.9995

VMEM = pl.BlockSpec(memory_space=pltpu.VMEM)
SMEM = pl.BlockSpec(memory_space=pltpu.SMEM)


def plan_kernel(own_blocks, half_blocks, live_ref, core_ref, coords_ref, tiles_hbm, *refs):
    cap = coords_ref.shape[1]
    out_refs, held_ref, sem = refs[:-2], refs[-2], refs[-1]
    load = pltpu.make_async_copy(tiles_hbm, held_ref, sem)
    load.start()
    width = out_refs[0].shape[1]
    follower = coords_ref[0:1, :]
    followee = coords_ref[1:2, :]
    slot = lax.broadcasted_iota(jnp.int32, (1, cap), 1)
    owner = follower // own_blocks
    inner = follower - owner * own_blocks
    near = (owner // CORES) * own_blocks + inner
    away = (owner % CORES) != core_ref[0]
    alive = slot < live_ref[0]
    earlier = (
        lax.broadcasted_iota(jnp.int32, (cap, cap), 0)
        < lax.broadcasted_iota(jnp.int32, (cap, cap), 1)
    )
    earlier = jnp.where(earlier, 1.0, 0.0).astype(jnp.bfloat16)
    below = (
        lax.broadcasted_iota(jnp.int32, (half_blocks, half_blocks), 1)
        < lax.broadcasted_iota(jnp.int32, (half_blocks, half_blocks), 0)
    )
    below = jnp.where(below, 1.0, 0.0).astype(jnp.bfloat16)
    block = lax.broadcasted_iota(jnp.int32, (half_blocks, cap), 0)
    place = lax.broadcasted_iota(jnp.int32, (width, cap), 0)
    spot = lax.broadcasted_iota(jnp.int32, (1, width), 1)
    for number, out_ref in enumerate(out_refs):
        forward, half = number < 2, number % 2
        source, target = (near, followee) if forward else (followee, near)
        member = jnp.logical_and(alive, away if half else jnp.logical_not(away))
        hit = jnp.where(jnp.logical_and(block == target, member), 1.0, 0.0)
        count = jnp.sum(hit, axis=1, keepdims=True)
        quads = jnp.floor((count + (QUAD - 1)) * (1.0 / QUAD))
        rank = jnp.dot(hit.astype(jnp.bfloat16), earlier, preferred_element_type=jnp.float32)
        wide = jnp.broadcast_to(quads, (half_blocks, SIDE)).astype(jnp.bfloat16)
        start = jnp.dot(below, wide, preferred_element_type=jnp.float32)[:, :1]
        position = jnp.sum(hit * (start * QUAD + rank), axis=0, keepdims=True)
        position = jnp.where(member, position.astype(jnp.int32), width)
        chosen = jnp.where(place == position, 1.0, 0.0).astype(jnp.bfloat16)
        rows = [slot // 2, slot % 2, half_blocks - source, target]
        rows += [jnp.zeros_like(slot)] * 4
        rows = jnp.concatenate(rows, axis=0).astype(jnp.float32).astype(jnp.bfloat16)
        listed = lax.dot_general(
            rows, chosen, (((1,), (1,)), ((), ())), preferred_element_type=jnp.float32
        ).astype(jnp.int32)
        code = (listed[0:1] * 2 + listed[1:2]) * FIELD + half_blocks - listed[2:3]
        code = code * FIELD + listed[3:4]
        total = jnp.sum(quads, axis=0, keepdims=True).astype(jnp.int32)
        out_ref[...] = jnp.where(spot == width - 1, total, code)
    load.wait()


def products_kernel(forward, based, coded, code_ref, panel_ref, tiles_ref, *refs):
    base_ref = refs[0] if based else None
    out_ref = refs[1 if based else 0]
    if coded:
        panel, total, most_ref, scale_ref = refs[-4:]
    else:
        panel, total = refs[-1], out_ref
    blocks = panel_ref.shape[0]
    count = code_ref[0, code_ref.shape[1] - 1]
    empty = jnp.zeros(total.shape[1:], jnp.float32)

    def clear(block, _):
        total[block] = base_ref[block] if based else empty
        panel[block] = panel_ref[block]
        return 0

    lax.fori_loop(0, blocks, clear, 0, unroll=4)
    panel[blocks] = jnp.zeros(panel.shape[1:], panel.dtype)

    def quad(number):
        tiles, picks = [], []
        for step in range(QUAD):
            code = code_ref[0, number * QUAD + step]
            picks.append(panel[lax.shift_right_logical(code, BITS) & (FIELD - 1)])
            tiles.append(tiles_ref[lax.shift_right_logical(code, 2 * BITS)])
        left = jnp.concatenate(picks, axis=1)
        right = jnp.concatenate(tiles, axis=0 if forward else 1)
        return lax.dot_general(
            left,
            right,
            (((1,), (0 if forward else 1,)), ((), ())),
            preferred_element_type=jnp.float32,
        )

    def body(number, _):
        first = number * UNROLL
        parts = [quad(first + step) for step in range(UNROLL)]
        for step in range(UNROLL):
            target = code_ref[0, (first + step) * QUAD] & (FIELD - 1)
            total[target] += parts[step]
        return 0

    lax.fori_loop(0, pl.cdiv(count, UNROLL), body, 0)
    if coded:
        encode(total, out_ref, most_ref, scale_ref)


def encode(total, out_ref, most_ref, scale_ref):
    targets = out_ref.shape[0]
    blocks, seeds, _ = total.shape
    own_blocks = blocks // targets
    for block in range(blocks):
        most_ref[block : block + 1, :] = jnp.max(jnp.abs(total[block]), axis=0, keepdims=True)
    power = jnp.floor(jnp.log2(jnp.maximum(most_ref[...], 1e-30) * 1.0001)) + 1.0
    scale_ref[...] = jnp.exp2(TOP - power) * MARGIN
    most_ref[...] = power
    for target in range(targets):
        for inner in range(own_blocks):
            block = target * own_blocks + inner
            coded = jnp.round(total[block] * scale_ref[block : block + 1, :])
            out_ref[target, inner * seeds : (inner + 1) * seeds, :] = coded.astype(
                jnp.int32
            ).astype(jnp.int16)
        tags = most_ref[target * own_blocks : (target + 1) * own_blocks, :]
        tags = jnp.concatenate([tags] * (TAG // own_blocks), axis=0)
        out_ref[target, own_blocks * seeds :, :] = tags.astype(jnp.int32).astype(jnp.int16)


def decoded(in_ref, source, inner, seeds):
    rows = in_ref.shape[1] - TAG
    coded = in_ref[source, inner * seeds : (inner + 1) * seeds, :]
    power = in_ref[source, rows : rows + TAG, :].astype(jnp.int32).astype(jnp.float32)
    power = power[inner : inner + 1]
    return coded.astype(jnp.int32).astype(jnp.float32) * (
        jnp.exp2(power - TOP) * (1.0 / MARGIN)
    )


def summed(in_ref, inner, seeds):
    value = decoded(in_ref, 0, inner, seeds)
    for source in range(1, in_ref.shape[0]):
        value = value + decoded(in_ref, source, inner, seeds)
    return value


def call(kernel, out, operands, scratch=(), specs=None, limit=SMALL):
    return pl.pallas_call(
        kernel,
        out_shape=out,
        in_specs=specs or [VMEM] * len(operands),
        out_specs=jax.tree.map(lambda _: VMEM, out),
        scratch_shapes=scratch,
        compiler_params=pltpu.CompilerParams(vmem_limit_bytes=limit),
    )(*operands)


def code_scratch(blocks, seeds):
    return [
        pltpu.VMEM((blocks, seeds, SIDE), jnp.float32),
        pltpu.VMEM((blocks, SIDE), jnp.float32),
        pltpu.VMEM((blocks, SIDE), jnp.float32),
    ]


def products(codes, panel, tile_values, own_blocks, forward, base=None, coded=True):
    blocks, seeds, _ = panel.shape
    targets = blocks // own_blocks
    scratch = [pltpu.VMEM((blocks + 1, seeds, SIDE), panel.dtype)]
    if coded:
        out = jax.ShapeDtypeStruct((targets, own_blocks * seeds + TAG, SIDE), jnp.int16)
        scratch += code_scratch(blocks, seeds)
    else:
        out = jax.ShapeDtypeStruct((blocks, seeds, SIDE), jnp.float32)
    operands = [codes, panel, tile_values] + ([] if base is None else [base])
    return call(
        functools.partial(products_kernel, forward, base is not None, coded),
        out,
        operands,
        scratch,
        [SMEM] + [VMEM] * (len(operands) - 1),
        LARGE,
    )


def join_kernel(own_ref, in_ref, out_ref, total, most_ref, scale_ref):
    blocks, seeds, _ = own_ref.shape
    own_blocks = blocks // in_ref.shape[0]
    for target in range(in_ref.shape[0]):
        for inner in range(own_blocks):
            block = target * own_blocks + inner
            total[block] = own_ref[block] + decoded(in_ref, target, inner, seeds)
    encode(total, out_ref, most_ref, scale_ref)


def join(own, other):
    blocks, seeds, _ = own.shape
    out = jax.ShapeDtypeStruct(other.shape, other.dtype)
    return call(join_kernel, out, [own, other], code_scratch(blocks, seeds))


def authority_kernel(in_ref, degree_ref, lent_ref, score_ref=None):
    copies, own_blocks, seeds, _ = lent_ref.shape
    for inner in range(own_blocks):
        degree = degree_ref[inner : inner + 1, :].astype(jnp.float32)
        score = summed(in_ref, inner, seeds) / degree
        lent = score.astype(jnp.bfloat16)
        for target in range(copies):
            lent_ref[target, inner] = lent
        if score_ref is not None:
            score_ref[inner * SIDE : (inner + 1) * SIDE, :] = jnp.transpose(score)


def hub_kernel(in_ref, seed_ref, first_ref, degree_ref, out_ref, last):
    own_blocks = degree_ref.shape[0]
    seeds = seed_ref.shape[1]
    wanted = jnp.broadcast_to(seed_ref[...].astype(jnp.float32), (SIDE, seeds))
    wanted = jnp.transpose(wanted).astype(jnp.int32)
    for inner in range(own_blocks):
        users = first_ref[0] + inner * SIDE + lax.broadcasted_iota(jnp.int32, (seeds, SIDE), 1)
        hit = jnp.where(users == wanted, 1.0, 0.0)
        hub = (1.0 - RESET) * summed(in_ref, inner, seeds) + RESET * hit
        if last:
            out_ref[inner * SIDE : (inner + 1) * SIDE, :] = jnp.transpose(hub)
        else:
            degree = degree_ref[inner : inner + 1, :].astype(jnp.float32)
            spread = (hub / degree).astype(jnp.bfloat16)
            for target in range(out_ref.shape[0]):
                out_ref[target, inner] = spread


def prior_kernel(hub_ref, degree_ref, out_ref):
    copies, own_blocks, _, _ = out_ref.shape
    for inner in range(own_blocks):
        hub = hub_ref[inner * SIDE : (inner + 1) * SIDE, :].astype(jnp.float32)
        degree = degree_ref[inner : inner + 1, :].astype(jnp.float32)
        spread = (jnp.transpose(hub) / degree).astype(jnp.bfloat16)
        for target in range(copies):
            out_ref[target, inner] = spread


def per_device(tile_values, tile_coords, tile_count, hub_prior, out_degree, in_degree, seed_ids):
    row_size = lax.axis_size("row")
    col_size = lax.axis_size("col")
    row_index = lax.axis_index("row")
    col_index = lax.axis_index("col")
    slice_rows = hub_prior.shape[0]
    own_blocks = slice_rows // SIDE
    chips = col_size // CORES
    half_blocks = chips * own_blocks
    cap = tile_values.shape[0]
    width = cap + QUAD * half_blocks
    seeds = seed_ids.shape[0]

    own_out = lax.dynamic_slice_in_dim(out_degree, col_index * slice_rows, slice_rows)
    own_out = own_out.reshape(own_blocks, SIDE)
    own_in = lax.dynamic_slice_in_dim(in_degree, row_index * slice_rows, slice_rows)
    own_in = own_in.reshape(own_blocks, SIDE)
    first_user = ((row_index * col_size + col_index) * slice_rows).astype(jnp.int32)[None]
    core = (col_index % CORES).astype(jnp.int32)[None]

    same_core = [[chip * CORES + k for chip in range(chips)] for k in range(CORES)]
    swap = [(c, c + 1 - 2 * (c % CORES)) for c in range(col_size)]

    def over_chips(parts):
        return lax.all_to_all(parts, "col", 0, 0, tiled=True, axis_index_groups=same_core)

    def over_rows(parts):
        return lax.all_to_all(parts, "row", 0, 0, tiled=True)

    code_type = jax.ShapeDtypeStruct((1, width), jnp.int32)
    to_near, to_away, from_near, from_away, tiles = call(
        functools.partial(plan_kernel, own_blocks, half_blocks),
        (code_type,) * 4 + (jax.ShapeDtypeStruct(tile_values.shape, tile_values.dtype),),
        [tile_count, core, tile_coords.T, tile_values],
        [pltpu.SemaphoreType.DMA(())],
        [SMEM, SMEM, VMEM, pl.BlockSpec(memory_space=pltpu.HBM)],
        LARGE,
    )

    def spread_type(copies):
        return jax.ShapeDtypeStruct((copies, own_blocks, seeds, SIDE), jnp.bfloat16)

    score_type = jax.ShapeDtypeStruct((slice_rows, seeds), jnp.float32)
    spread = call(prior_kernel, spread_type(chips), [hub_prior, own_out])
    (spread, to_near, to_away, from_near, from_away, tiles, own_out, own_in, first_user) = (
        lax.optimization_barrier(
            (
                spread,
                to_near,
                to_away,
                from_near,
                from_away,
                tiles,
                own_out,
                own_in,
                first_user,
            )
        )
    )
    for sweep_number in range(SWEEPS):
        last = sweep_number + 1 == SWEEPS
        near = over_chips(spread).reshape(half_blocks, seeds, SIDE)
        away = lax.ppermute(near, "col", swap)
        partial = products(to_near, near, tiles, own_blocks, True, coded=False)
        partial = products(to_away, away, tiles, own_blocks, True, base=partial)
        out = (spread_type(row_size), score_type) if last else (spread_type(row_size),)
        lent = call(authority_kernel, out, [over_rows(partial), own_in])
        panel = over_rows(lent[0]).reshape(half_blocks, seeds, SIDE)
        theirs = products(from_away, panel, tiles, own_blocks, False)
        theirs = lax.ppermute(theirs, "col", swap)
        mine = products(from_near, panel, tiles, own_blocks, False, coded=False)
        spread = call(
            functools.partial(hub_kernel, last=last),
            score_type if last else spread_type(chips),
            [over_chips(join(mine, theirs)), seed_ids[None, :], first_user, own_out],
            specs=[VMEM, VMEM, SMEM, VMEM],
        )
    return (spread, lent[1])


def solution(mesh):
    placed = (
        P(("row", "col"), None, None),
        P(("row", "col"), None),
        P(("row", "col")),
        P(("row", "col"), None),
        P("row"),
        P("col"),
        P(),
    )
    return jax.shard_map(
        per_device,
        mesh=mesh,
        in_specs=placed,
        out_specs=(P(("row", "col"), None), P(("col", "row"), None)),
        check_vma=False,
    )
```

```python
import functools

import jax
import jax.numpy as jnp
from jax import lax
from jax.experimental import pallas as pl
from jax.experimental.pallas import tpu as pltpu
from jax.sharding import PartitionSpec as P

SWEEPS = 2
RESET = 0.3
SIDE = 128
CORES = 2
GROUP = 2
LOADS = 8
LATE = 5000
LATE_JOIN = 3000
UNROLL = 16
BITS = 6
FIELD = 1 << BITS
SMALL = 8 << 20
LARGE = 24 << 20
TAG = 16
TOP = 15
MARGIN = 0.9995

VMEM = pl.BlockSpec(memory_space=pltpu.VMEM)
SMEM = pl.BlockSpec(memory_space=pltpu.SMEM)


def spread_out(hub, degree_ref, inner, own_blocks, out_ref):
    copies = out_ref.shape[0]
    seeds = hub.shape[0]
    place = lax.axis_index("col") * own_blocks + inner
    spread = (hub / degree_ref[pl.ds(place, 1), :].astype(jnp.float32)).astype(jnp.bfloat16)
    for target in range(copies):
        out_ref[target, inner * seeds : (inner + 1) * seeds, :] = spread


def tag_out(value, out_ref):
    copies, rows, _ = out_ref.shape
    for target in range(copies):
        out_ref[target, rows - TAG :, :] = jnp.broadcast_to(value, (TAG, SIDE)).astype(
            out_ref.dtype
        )


def start_kernel(half_blocks, live_ref, coords_ref, hub_ref, degree_ref, tiles_hbm, *refs):
    cap = coords_ref.shape[1]
    out_refs, (held_ref, spread_ref, sem) = refs[:-3], refs[-3:]
    step = cap // LOADS
    loads = []
    for number in range(LOADS):
        rows = pl.ds(number * step, step)
        load = pltpu.make_async_copy(tiles_hbm.at[rows], held_ref.at[rows], sem.at[number])
        loads.append((number * step < live_ref[0], load))
    for live, load in loads:
        pl.when(live)(load.start)
    held_ref[cap] = jnp.zeros(held_ref.shape[1:], held_ref.dtype)
    own_blocks = hub_ref.shape[0] // SIDE
    tag_out((live_ref[0] // 2).astype(jnp.float32), spread_ref)
    for inner in range(own_blocks):
        hub = hub_ref[inner * SIDE : (inner + 1) * SIDE, :].astype(jnp.float32)
        spread_out(jnp.transpose(hub), degree_ref, inner, own_blocks, spread_ref)
    width = out_refs[0].shape[1]
    follower = coords_ref[0:1, :]
    followee = coords_ref[1:2, :]
    slot = lax.broadcasted_iota(jnp.int32, (1, cap), 1)
    owner = follower // own_blocks
    inner = follower - owner * own_blocks
    near = (owner // CORES) * own_blocks + inner
    away = (owner % CORES) != lax.axis_index("col") % CORES
    alive = slot < live_ref[0]
    earlier = (
        lax.broadcasted_iota(jnp.int32, (cap, cap), 0)
        < lax.broadcasted_iota(jnp.int32, (cap, cap), 1)
    )
    earlier = jnp.where(earlier, 1.0, 0.0).astype(jnp.bfloat16)
    below = (
        lax.broadcasted_iota(jnp.int32, (half_blocks, half_blocks), 1)
        < lax.broadcasted_iota(jnp.int32, (half_blocks, half_blocks), 0)
    )
    below = jnp.where(below, 1.0, 0.0).astype(jnp.bfloat16)
    block = lax.broadcasted_iota(jnp.int32, (half_blocks, cap), 0)
    place = lax.broadcasted_iota(jnp.int32, (width, cap), 0)
    spot = lax.broadcasted_iota(jnp.int32, (1, width), 1)
    for number, out_ref in enumerate(out_refs):
        forward, half = number < 2, number % 2
        source, target = (near, followee) if forward else (followee, near)
        member = jnp.logical_and(alive, away if half else jnp.logical_not(away))
        hit = jnp.where(jnp.logical_and(block == target, member), 1.0, 0.0)
        count = jnp.sum(hit, axis=1, keepdims=True)
        groups = jnp.floor((count + (GROUP - 1)) * (1.0 / GROUP))
        rank = jnp.dot(hit.astype(jnp.bfloat16), earlier, preferred_element_type=jnp.float32)
        wide = jnp.broadcast_to(groups, (half_blocks, SIDE)).astype(jnp.bfloat16)
        start = jnp.dot(below, wide, preferred_element_type=jnp.float32)[:, :1]
        position = jnp.sum(hit * (start * GROUP + rank), axis=0, keepdims=True)
        position = jnp.where(member, position.astype(jnp.int32), width)
        chosen = jnp.where(place == position, 1.0, 0.0).astype(jnp.bfloat16)
        rows = [(cap - slot) // 2, (cap - slot) % 2, source, target]
        rows += [jnp.zeros_like(slot)] * 4
        rows = jnp.concatenate(rows, axis=0).astype(jnp.float32).astype(jnp.bfloat16)
        listed = lax.dot_general(
            rows, chosen, (((1,), (1,)), ((), ())), preferred_element_type=jnp.float32
        ).astype(jnp.int32)
        code = (cap - listed[0:1] * 2 - listed[1:2]) * FIELD + listed[2:3]
        code = code * FIELD + listed[3:4]
        total = jnp.sum(groups, axis=0, keepdims=True).astype(jnp.int32)
        out_ref[...] = jnp.where(spot == width - 1, total, code)
    for live, load in loads:
        pl.when(live)(load.wait)


def products_kernel(forward, based, coded, own_blocks, code_ref, panel_ref, tiles_ref, *refs):
    base_ref, late_ref = refs[:2] if based else (None, None)
    out_ref = refs[2 if based else 0]
    if coded:
        total, most_ref, scale_ref = refs[-3:]
    else:
        total = out_ref
    blocks = total.shape[0]
    seeds = total.shape[1]
    count = code_ref[0, code_ref.shape[1] - 1]
    empty = jnp.zeros(total.shape[1:], jnp.float32)

    def clear(block, _):
        total[block] = base_ref[block] if based else empty
        return 0

    lax.fori_loop(0, blocks, clear, 0, unroll=4)

    def quad(number):
        tiles, picks = [], []
        for step in range(GROUP):
            code = code_ref[0, number * GROUP + step]
            source = lax.shift_right_logical(code, BITS) & (FIELD - 1)
            if forward:
                first = pl.multiple_of((source & (own_blocks - 1)) * seeds, seeds)
                chip = lax.shift_right_logical(source, own_blocks.bit_length() - 1)
                picks.append(panel_ref[chip, pl.ds(first, seeds), :])
            else:
                picks.append(panel_ref[source])
            tiles.append(tiles_ref[lax.shift_right_logical(code, 2 * BITS)])
        left = jnp.concatenate(picks, axis=1)
        right = jnp.concatenate(tiles, axis=0 if forward else 1)
        return lax.dot_general(
            left,
            right,
            (((1,), (0 if forward else 1,)), ((), ())),
            preferred_element_type=jnp.float32,
        )

    def body(number, _):
        first = number * UNROLL
        parts = [quad(first + step) for step in range(UNROLL)]
        for step in range(UNROLL):
            target = code_ref[0, (first + step) * GROUP] & (FIELD - 1)
            total[target] += parts[step]
        return 0

    lax.fori_loop(0, pl.cdiv(count, UNROLL), body, 0)
    if coded:
        encode(total, out_ref, most_ref, scale_ref)
    if based:
        stagger(late_ref, LATE)


def encode(total, out_ref, most_ref, scale_ref):
    targets = out_ref.shape[0]
    blocks, seeds, _ = total.shape
    own_blocks = blocks // targets
    for block in range(blocks):
        most_ref[block : block + 1, :] = jnp.max(jnp.abs(total[block]), axis=0, keepdims=True)
    power = jnp.floor(jnp.log2(jnp.maximum(most_ref[...], 1e-30) * 1.0001)) + 1.0
    scale_ref[...] = jnp.exp2(TOP - power) * MARGIN
    most_ref[...] = power
    for target in range(targets):
        for inner in range(own_blocks):
            block = target * own_blocks + inner
            coded = jnp.round(total[block] * scale_ref[block : block + 1, :])
            out_ref[target, inner * seeds : (inner + 1) * seeds, :] = coded.astype(
                jnp.int32
            ).astype(jnp.int16)
        tags = most_ref[target * own_blocks : (target + 1) * own_blocks, :]
        tags = jnp.concatenate([tags] * (TAG // own_blocks), axis=0)
        out_ref[target, own_blocks * seeds :, :] = tags.astype(jnp.int32).astype(jnp.int16)


def decoded(in_ref, source, inner, seeds):
    rows = in_ref.shape[1] - TAG
    coded = in_ref[source, inner * seeds : (inner + 1) * seeds, :]
    power = in_ref[source, rows : rows + TAG, :].astype(jnp.int32).astype(jnp.float32)
    power = power[inner : inner + 1]
    return coded.astype(jnp.int32).astype(jnp.float32) * (
        jnp.exp2(power - TOP) * (1.0 / MARGIN)
    )


def summed(in_ref, inner, seeds):
    value = decoded(in_ref, 0, inner, seeds)
    for source in range(1, in_ref.shape[0]):
        value = value + decoded(in_ref, source, inner, seeds)
    return value


def call(kernel, out, operands, scratch=(), specs=None, limit=SMALL, out_specs=None):
    return pl.pallas_call(
        kernel,
        out_shape=out,
        in_specs=specs or [VMEM] * len(operands),
        out_specs=out_specs or jax.tree.map(lambda _: VMEM, out),
        scratch_shapes=scratch,
        compiler_params=pltpu.CompilerParams(vmem_limit_bytes=limit),
    )(*operands)


def code_scratch(blocks, seeds):
    return [
        pltpu.VMEM((blocks, seeds, SIDE), jnp.float32),
        pltpu.VMEM((blocks, SIDE), jnp.float32),
        pltpu.VMEM((blocks, SIDE), jnp.float32),
    ]


def products(codes, panel, tile_values, own_blocks, forward, base=(), coded=True):
    if forward:
        blocks, seeds = panel.shape[0] * own_blocks, (panel.shape[1] - TAG) // own_blocks
    else:
        blocks, seeds, _ = panel.shape
    targets = blocks // own_blocks
    scratch = []
    if coded:
        out = jax.ShapeDtypeStruct((targets, own_blocks * seeds + TAG, SIDE), jnp.int16)
        scratch += code_scratch(blocks, seeds)
    else:
        out = jax.ShapeDtypeStruct((blocks, seeds, SIDE), jnp.float32)
    operands = [codes, panel, tile_values, *base]
    return call(
        functools.partial(products_kernel, forward, bool(base), coded, own_blocks),
        out,
        operands,
        scratch,
        [SMEM, VMEM, VMEM] + ([VMEM, SMEM] if base else []),
        LARGE,
    )


def join_kernel(own_ref, in_ref, late_ref, out_ref, total, most_ref, scale_ref):
    blocks, seeds, _ = own_ref.shape
    own_blocks = blocks // in_ref.shape[0]
    for target in range(in_ref.shape[0]):
        for inner in range(own_blocks):
            block = target * own_blocks + inner
            total[block] = own_ref[block] + decoded(in_ref, target, inner, seeds)
    encode(total, out_ref, most_ref, scale_ref)
    stagger(late_ref, LATE_JOIN)


def join(own, other, late):
    blocks, seeds, _ = own.shape
    out = jax.ShapeDtypeStruct(other.shape, other.dtype)
    return call(
        join_kernel, out, [own, other, late], code_scratch(blocks, seeds), [VMEM, VMEM, SMEM]
    )


def authority_kernel(in_ref, degree_ref, lent_ref, score_ref=None):
    copies, own_blocks, seeds, _ = lent_ref.shape
    for inner in range(own_blocks):
        place = lax.axis_index("row") * own_blocks + inner
        degree = degree_ref[pl.ds(place, 1), :].astype(jnp.float32)
        score = summed(in_ref, inner, seeds) / degree
        lent = score.astype(jnp.bfloat16)
        for target in range(copies):
            lent_ref[target, inner] = lent
        if score_ref is not None:
            score_ref[inner * SIDE : (inner + 1) * SIDE, :] = jnp.transpose(score)


def late_kernel(near_ref, away_ref, live_ref, late_ref):
    rows = near_ref.shape[1]
    near = jnp.max(near_ref[:, rows - TAG :, :].astype(jnp.float32))
    away = jnp.max(away_ref[:, rows - TAG :, :].astype(jnp.float32))
    odd = lax.axis_index("col") % CORES == 1
    heavier = jnp.logical_or(near > away, jnp.logical_and(near == away, odd))
    own = (live_ref[0] // 2).astype(jnp.float32)
    light = jnp.logical_or(own * 2.0 < near, odd)
    late_ref[0] = jnp.logical_and(heavier, light).astype(jnp.int32)


def stagger(late_ref, nanos):
    @pl.when(late_ref[0] == 1)
    def _():
        pl.delay(nanos)


def hub_kernel(last, own_blocks, in_ref, seed_ref, degree_ref, out_ref):
    if not last:
        tag_out(jnp.zeros((), jnp.float32), out_ref)
    seeds = seed_ref.shape[1]
    wanted = jnp.broadcast_to(seed_ref[...].astype(jnp.float32), (SIDE, seeds))
    wanted = jnp.transpose(wanted).astype(jnp.int32)
    device = lax.axis_index("row") * lax.axis_size("col") + lax.axis_index("col")
    for inner in range(own_blocks):
        first = (device * own_blocks + inner) * SIDE
        users = first + lax.broadcasted_iota(jnp.int32, (seeds, SIDE), 1)
        hit = jnp.where(users == wanted, 1.0, 0.0)
        hub = (1.0 - RESET) * summed(in_ref, inner, seeds) + RESET * hit
        if last:
            out_ref[inner * SIDE : (inner + 1) * SIDE, :] = jnp.transpose(hub)
        else:
            spread_out(hub, degree_ref, inner, own_blocks, out_ref)


def per_device(tile_values, tile_coords, tile_count, hub_prior, out_degree, in_degree, seed_ids):
    row_size = lax.axis_size("row")
    col_size = lax.axis_size("col")
    slice_rows = hub_prior.shape[0]
    own_blocks = slice_rows // SIDE
    chips = col_size // CORES
    half_blocks = chips * own_blocks
    cap = tile_values.shape[0]
    width = pl.cdiv(cap + GROUP * half_blocks, SIDE) * SIDE
    seeds = seed_ids.shape[0]
    out_degree = out_degree.reshape(-1, SIDE)
    in_degree = in_degree.reshape(-1, SIDE)

    same_core = [[chip * CORES + k for chip in range(chips)] for k in range(CORES)]
    swap = [(c, c + 1 - 2 * (c % CORES)) for c in range(col_size)]

    def over_chips(parts):
        return lax.all_to_all(parts, "col", 0, 0, tiled=True, axis_index_groups=same_core)

    def over_rows(parts):
        return lax.all_to_all(parts, "row", 0, 0, tiled=True)

    def spread_type(copies):
        return jax.ShapeDtypeStruct((copies, own_blocks, seeds, SIDE), jnp.bfloat16)

    panel_type = jax.ShapeDtypeStruct((chips, own_blocks * seeds + TAG, SIDE), jnp.bfloat16)
    score_type = jax.ShapeDtypeStruct((slice_rows, seeds), jnp.float32)
    code_type = jax.ShapeDtypeStruct((1, width), jnp.int32)
    held_type = jax.ShapeDtypeStruct((cap + 1, SIDE, SIDE), tile_values.dtype)
    tile_values = pltpu.with_memory_space_constraint(tile_values, pltpu.HBM)
    to_near, to_away, from_near, from_away, tiles, spread = call(
        functools.partial(start_kernel, half_blocks),
        (code_type,) * 4 + (held_type, panel_type),
        [tile_count, tile_coords.T, hub_prior, out_degree, tile_values],
        [pltpu.SemaphoreType.DMA((LOADS,))],
        [SMEM, VMEM, VMEM, VMEM, pl.BlockSpec(memory_space=pltpu.HBM)],
        LARGE,
    )

    for sweep_number in range(SWEEPS):
        last = sweep_number + 1 == SWEEPS
        near = over_chips(spread)
        away = lax.ppermute(near, "col", swap)
        partial = products(to_near, near, tiles, own_blocks, True, coded=False)
        if sweep_number == 0:
            late = call(
                late_kernel,
                jax.ShapeDtypeStruct((1,), jnp.int32),
                [near, away, tile_count],
                specs=[VMEM, VMEM, SMEM],
                out_specs=SMEM,
            )
        partial = products(to_away, away, tiles, own_blocks, True, base=(partial, late))
        out = (spread_type(row_size), score_type) if last else (spread_type(row_size),)
        lent = call(authority_kernel, out, [over_rows(partial), in_degree])
        panel = over_rows(lent[0]).reshape(half_blocks, seeds, SIDE)
        theirs = products(from_away, panel, tiles, own_blocks, False)
        theirs = lax.ppermute(theirs, "col", swap)
        mine = products(from_near, panel, tiles, own_blocks, False, coded=False)
        spread = call(
            functools.partial(hub_kernel, last, own_blocks),
            score_type if last else panel_type,
            [over_chips(join(mine, theirs, late)), seed_ids[None, :], out_degree],
        )
    return (spread, lent[1])


def solution(mesh):
    placed = (
        P(("row", "col"), None, None),
        P(("row", "col"), None),
        P(("row", "col")),
        P(("row", "col"), None),
        P("row"),
        P("col"),
        P(),
    )
    return jax.shard_map(
        per_device,
        mesh=mesh,
        in_specs=placed,
        out_specs=(P(("row", "col"), None), P(("col", "row"), None)),
        check_vma=False,
    )
```

```python
import functools

import jax
import jax.numpy as jnp
from jax import lax
from jax.experimental import pallas as pl
from jax.experimental.pallas import tpu as pltpu
from jax.sharding import PartitionSpec as P

SWEEPS = 2
RESET = 0.3
SIDE = 128
CORES = 2
GROUP = 2
LOADS = 8
LATE = 5000
LATE_JOIN = 4500
UNROLL = 16
BITS = 6
FIELD = 1 << BITS
SMALL = 8 << 20
LARGE = 24 << 20
TAG = 16
TOP = 15
MARGIN = 0.9995

VMEM = pl.BlockSpec(memory_space=pltpu.VMEM)
SMEM = pl.BlockSpec(memory_space=pltpu.SMEM)


def spread_out(hub, degree_ref, inner, own_blocks, out_ref):
    copies = out_ref.shape[0]
    seeds = hub.shape[0]
    place = lax.axis_index("col") * own_blocks + inner
    spread = (hub / degree_ref[pl.ds(place, 1), :].astype(jnp.float32)).astype(jnp.bfloat16)
    for target in range(copies):
        out_ref[target, inner * seeds : (inner + 1) * seeds, :] = spread


def tag_out(value, out_ref):
    copies, rows, _ = out_ref.shape
    for target in range(copies):
        out_ref[target, rows - TAG :, :] = jnp.broadcast_to(value, (TAG, SIDE)).astype(
            out_ref.dtype
        )


def start_kernel(half_blocks, live_ref, coords_ref, hub_ref, degree_ref, tiles_hbm, *refs):
    cap = coords_ref.shape[1]
    out_refs, (held_ref, spread_ref, sem) = refs[:-3], refs[-3:]
    step = cap // LOADS
    loads = []
    for number in range(LOADS):
        rows = pl.ds(number * step, step)
        load = pltpu.make_async_copy(tiles_hbm.at[rows], held_ref.at[rows], sem.at[number])
        loads.append((number * step < live_ref[0], load))
    for live, load in loads:
        pl.when(live)(load.start)
    held_ref[cap] = jnp.zeros(held_ref.shape[1:], held_ref.dtype)
    own_blocks = hub_ref.shape[0] // SIDE
    tag_out((live_ref[0] // 2).astype(jnp.float32), spread_ref)
    for inner in range(own_blocks):
        hub = hub_ref[inner * SIDE : (inner + 1) * SIDE, :].astype(jnp.float32)
        spread_out(jnp.transpose(hub), degree_ref, inner, own_blocks, spread_ref)
    width = out_refs[0].shape[1]
    follower = coords_ref[0:1, :]
    followee = coords_ref[1:2, :]
    slot = lax.broadcasted_iota(jnp.int32, (1, cap), 1)
    owner = follower // own_blocks
    inner = follower - owner * own_blocks
    near = (owner // CORES) * own_blocks + inner
    away = (owner % CORES) != lax.axis_index("col") % CORES
    alive = slot < live_ref[0]
    earlier = (
        lax.broadcasted_iota(jnp.int32, (cap, cap), 0)
        < lax.broadcasted_iota(jnp.int32, (cap, cap), 1)
    )
    earlier = jnp.where(earlier, 1.0, 0.0).astype(jnp.bfloat16)
    below = (
        lax.broadcasted_iota(jnp.int32, (half_blocks, half_blocks), 1)
        < lax.broadcasted_iota(jnp.int32, (half_blocks, half_blocks), 0)
    )
    below = jnp.where(below, 1.0, 0.0).astype(jnp.bfloat16)
    block = lax.broadcasted_iota(jnp.int32, (half_blocks, cap), 0)
    place = lax.broadcasted_iota(jnp.int32, (width, cap), 0)
    spot = lax.broadcasted_iota(jnp.int32, (1, width), 1)
    for number, out_ref in enumerate(out_refs):
        forward, half = number < 2, number % 2
        source, target = (near, followee) if forward else (followee, near)
        member = jnp.logical_and(alive, away if half else jnp.logical_not(away))
        hit = jnp.where(jnp.logical_and(block == target, member), 1.0, 0.0)
        count = jnp.sum(hit, axis=1, keepdims=True)
        groups = jnp.floor((count + (GROUP - 1)) * (1.0 / GROUP))
        rank = jnp.dot(hit.astype(jnp.bfloat16), earlier, preferred_element_type=jnp.float32)
        wide = jnp.broadcast_to(groups, (half_blocks, SIDE)).astype(jnp.bfloat16)
        start = jnp.dot(below, wide, preferred_element_type=jnp.float32)[:, :1]
        position = jnp.sum(hit * (start * GROUP + rank), axis=0, keepdims=True)
        position = jnp.where(member, position.astype(jnp.int32), width)
        chosen = jnp.where(place == position, 1.0, 0.0).astype(jnp.bfloat16)
        rows = [(cap - slot) // 2, (cap - slot) % 2, source, target]
        rows += [jnp.zeros_like(slot)] * 4
        rows = jnp.concatenate(rows, axis=0).astype(jnp.float32).astype(jnp.bfloat16)
        listed = lax.dot_general(
            rows, chosen, (((1,), (1,)), ((), ())), preferred_element_type=jnp.float32
        ).astype(jnp.int32)
        code = (cap - listed[0:1] * 2 - listed[1:2]) * FIELD + listed[2:3]
        code = code * FIELD + listed[3:4]
        total = jnp.sum(groups, axis=0, keepdims=True).astype(jnp.int32)
        out_ref[...] = jnp.where(spot == width - 1, total, code)
    for live, load in loads:
        pl.when(live)(load.wait)


def products_kernel(forward, based, coded, own_blocks, code_ref, panel_ref, tiles_ref, *refs):
    base_ref, late_ref = refs[:2] if based else (None, None)
    out_ref = refs[2 if based else 0]
    if coded:
        total, most_ref, scale_ref = refs[-3:]
    else:
        total = out_ref
    blocks = total.shape[0]
    seeds = total.shape[1]
    count = code_ref[0, code_ref.shape[1] - 1]
    empty = jnp.zeros(total.shape[1:], jnp.float32)

    def clear(block, _):
        total[block] = base_ref[block] if based else empty
        return 0

    lax.fori_loop(0, blocks, clear, 0, unroll=4)

    def quad(number):
        tiles, picks = [], []
        for step in range(GROUP):
            code = code_ref[0, number * GROUP + step]
            source = lax.shift_right_logical(code, BITS) & (FIELD - 1)
            if forward:
                first = pl.multiple_of((source & (own_blocks - 1)) * seeds, seeds)
                chip = lax.shift_right_logical(source, own_blocks.bit_length() - 1)
                picks.append(panel_ref[chip, pl.ds(first, seeds), :])
            else:
                picks.append(panel_ref[source])
            tiles.append(tiles_ref[lax.shift_right_logical(code, 2 * BITS)])
        left = jnp.concatenate(picks, axis=1)
        right = jnp.concatenate(tiles, axis=0 if forward else 1)
        return lax.dot_general(
            left,
            right,
            (((1,), (0 if forward else 1,)), ((), ())),
            preferred_element_type=jnp.float32,
        )

    def body(number, _):
        first = number * UNROLL
        parts = [quad(first + step) for step in range(UNROLL)]
        for step in range(UNROLL):
            target = code_ref[0, (first + step) * GROUP] & (FIELD - 1)
            total[target] += parts[step]
        return 0

    lax.fori_loop(0, pl.cdiv(count, UNROLL), body, 0)
    if coded:
        encode(total, out_ref, most_ref, scale_ref)
    if based:
        stagger(late_ref, LATE)


def encode(total, out_ref, most_ref, scale_ref):
    targets = out_ref.shape[0]
    blocks, seeds, _ = total.shape
    own_blocks = blocks // targets
    for block in range(blocks):
        most_ref[block : block + 1, :] = jnp.max(jnp.abs(total[block]), axis=0, keepdims=True)
    power = jnp.floor(jnp.log2(jnp.maximum(most_ref[...], 1e-30) * 1.0001)) + 1.0
    scale_ref[...] = jnp.exp2(TOP - power) * MARGIN
    most_ref[...] = power
    for target in range(targets):
        for inner in range(own_blocks):
            block = target * own_blocks + inner
            coded = jnp.round(total[block] * scale_ref[block : block + 1, :])
            out_ref[target, inner * seeds : (inner + 1) * seeds, :] = coded.astype(
                jnp.int32
            ).astype(jnp.int16)
        tags = most_ref[target * own_blocks : (target + 1) * own_blocks, :]
        tags = jnp.concatenate([tags] * (TAG // own_blocks), axis=0)
        out_ref[target, own_blocks * seeds :, :] = tags.astype(jnp.int32).astype(jnp.int16)


def decoded(in_ref, source, inner, seeds):
    rows = in_ref.shape[1] - TAG
    coded = in_ref[source, inner * seeds : (inner + 1) * seeds, :]
    power = in_ref[source, rows : rows + TAG, :].astype(jnp.int32).astype(jnp.float32)
    power = power[inner : inner + 1]
    return coded.astype(jnp.int32).astype(jnp.float32) * (
        jnp.exp2(power - TOP) * (1.0 / MARGIN)
    )


def summed(in_ref, inner, seeds):
    value = decoded(in_ref, 0, inner, seeds)
    for source in range(1, in_ref.shape[0]):
        value = value + decoded(in_ref, source, inner, seeds)
    return value


def call(kernel, out, operands, scratch=(), specs=None, limit=SMALL, out_specs=None):
    return pl.pallas_call(
        kernel,
        out_shape=out,
        in_specs=specs or [VMEM] * len(operands),
        out_specs=out_specs or jax.tree.map(lambda _: VMEM, out),
        scratch_shapes=scratch,
        compiler_params=pltpu.CompilerParams(vmem_limit_bytes=limit),
    )(*operands)


def code_scratch(blocks, seeds):
    return [
        pltpu.VMEM((blocks, seeds, SIDE), jnp.float32),
        pltpu.VMEM((blocks, SIDE), jnp.float32),
        pltpu.VMEM((blocks, SIDE), jnp.float32),
    ]


def products(codes, panel, tile_values, own_blocks, forward, base=(), coded=True):
    if forward:
        blocks, seeds = panel.shape[0] * own_blocks, (panel.shape[1] - TAG) // own_blocks
    else:
        blocks, seeds, _ = panel.shape
    targets = blocks // own_blocks
    scratch = []
    if coded:
        out = jax.ShapeDtypeStruct((targets, own_blocks * seeds + TAG, SIDE), jnp.int16)
        scratch += code_scratch(blocks, seeds)
    else:
        out = jax.ShapeDtypeStruct((blocks, seeds, SIDE), jnp.float32)
    operands = [codes, panel, tile_values, *base]
    return call(
        functools.partial(products_kernel, forward, bool(base), coded, own_blocks),
        out,
        operands,
        scratch,
        [SMEM, VMEM, VMEM] + ([VMEM, SMEM] if base else []),
        LARGE,
    )


def join_kernel(nanos, own_ref, in_ref, late_ref, out_ref, total, most_ref, scale_ref):
    blocks, seeds, _ = own_ref.shape
    own_blocks = blocks // in_ref.shape[0]
    for target in range(in_ref.shape[0]):
        for inner in range(own_blocks):
            block = target * own_blocks + inner
            total[block] = own_ref[block] + decoded(in_ref, target, inner, seeds)
    encode(total, out_ref, most_ref, scale_ref)
    if nanos:
        stagger(late_ref, nanos)


def join(own, other, late, nanos):
    blocks, seeds, _ = own.shape
    out = jax.ShapeDtypeStruct(other.shape, other.dtype)
    return call(
        functools.partial(join_kernel, nanos), out, [own, other, late], code_scratch(blocks, seeds), [VMEM, VMEM, SMEM]
    )


def authority_kernel(in_ref, degree_ref, lent_ref, score_ref=None):
    copies, own_blocks, seeds, _ = lent_ref.shape
    for inner in range(own_blocks):
        place = lax.axis_index("row") * own_blocks + inner
        degree = degree_ref[pl.ds(place, 1), :].astype(jnp.float32)
        score = summed(in_ref, inner, seeds) / degree
        lent = score.astype(jnp.bfloat16)
        for target in range(copies):
            lent_ref[target, inner] = lent
        if score_ref is not None:
            score_ref[inner * SIDE : (inner + 1) * SIDE, :] = jnp.transpose(score)


def late_kernel(near_ref, away_ref, live_ref, late_ref):
    rows = near_ref.shape[1]
    near = jnp.max(near_ref[:, rows - TAG :, :].astype(jnp.float32))
    away = jnp.max(away_ref[:, rows - TAG :, :].astype(jnp.float32))
    odd = lax.axis_index("col") % CORES == 1
    heavier = jnp.logical_or(near > away, jnp.logical_and(near == away, odd))
    own = (live_ref[0] // 2).astype(jnp.float32)
    light = jnp.logical_or(own * 2.0 < near, odd)
    late_ref[0] = jnp.logical_and(heavier, light).astype(jnp.int32)


def stagger(late_ref, nanos):
    @pl.when(late_ref[0] == 1)
    def _():
        pl.delay(nanos)


def hub_kernel(last, own_blocks, in_ref, seed_ref, degree_ref, out_ref):
    if not last:
        tag_out(jnp.zeros((), jnp.float32), out_ref)
    seeds = seed_ref.shape[1]
    wanted = jnp.broadcast_to(seed_ref[...].astype(jnp.float32), (SIDE, seeds))
    wanted = jnp.transpose(wanted).astype(jnp.int32)
    device = lax.axis_index("row") * lax.axis_size("col") + lax.axis_index("col")
    for inner in range(own_blocks):
        first = (device * own_blocks + inner) * SIDE
        users = first + lax.broadcasted_iota(jnp.int32, (seeds, SIDE), 1)
        hit = jnp.where(users == wanted, 1.0, 0.0)
        hub = (1.0 - RESET) * summed(in_ref, inner, seeds) + RESET * hit
        if last:
            out_ref[inner * SIDE : (inner + 1) * SIDE, :] = jnp.transpose(hub)
        else:
            spread_out(hub, degree_ref, inner, own_blocks, out_ref)


def per_device(tile_values, tile_coords, tile_count, hub_prior, out_degree, in_degree, seed_ids):
    row_size = lax.axis_size("row")
    col_size = lax.axis_size("col")
    slice_rows = hub_prior.shape[0]
    own_blocks = slice_rows // SIDE
    chips = col_size // CORES
    half_blocks = chips * own_blocks
    cap = tile_values.shape[0]
    width = pl.cdiv(cap + GROUP * half_blocks, SIDE) * SIDE
    seeds = seed_ids.shape[0]
    out_degree = out_degree.reshape(-1, SIDE)
    in_degree = in_degree.reshape(-1, SIDE)

    same_core = [[chip * CORES + k for chip in range(chips)] for k in range(CORES)]
    swap = [(c, c + 1 - 2 * (c % CORES)) for c in range(col_size)]

    def over_chips(parts):
        return lax.all_to_all(parts, "col", 0, 0, tiled=True, axis_index_groups=same_core)

    def over_rows(parts):
        return lax.all_to_all(parts, "row", 0, 0, tiled=True)

    def spread_type(copies):
        return jax.ShapeDtypeStruct((copies, own_blocks, seeds, SIDE), jnp.bfloat16)

    panel_type = jax.ShapeDtypeStruct((chips, own_blocks * seeds + TAG, SIDE), jnp.bfloat16)
    score_type = jax.ShapeDtypeStruct((slice_rows, seeds), jnp.float32)
    code_type = jax.ShapeDtypeStruct((1, width), jnp.int32)
    held_type = jax.ShapeDtypeStruct((cap + 1, SIDE, SIDE), tile_values.dtype)
    tile_values = pltpu.with_memory_space_constraint(tile_values, pltpu.HBM)
    to_near, to_away, from_near, from_away, tiles, spread = call(
        functools.partial(start_kernel, half_blocks),
        (code_type,) * 4 + (held_type, panel_type),
        [tile_count, tile_coords.T, hub_prior, out_degree, tile_values],
        [pltpu.SemaphoreType.DMA((LOADS,))],
        [SMEM, VMEM, VMEM, VMEM, pl.BlockSpec(memory_space=pltpu.HBM)],
        LARGE,
    )

    for sweep_number in range(SWEEPS):
        last = sweep_number + 1 == SWEEPS
        near = over_chips(spread)
        away = lax.ppermute(near, "col", swap)
        partial = products(to_near, near, tiles, own_blocks, True, coded=False)
        if sweep_number == 0:
            late = call(
                late_kernel,
                jax.ShapeDtypeStruct((1,), jnp.int32),
                [near, away, tile_count],
                specs=[VMEM, VMEM, SMEM],
                out_specs=SMEM,
            )
        partial = products(to_away, away, tiles, own_blocks, True, base=(partial, late))
        out = (spread_type(row_size), score_type) if last else (spread_type(row_size),)
        lent = call(authority_kernel, out, [over_rows(partial), in_degree])
        panel = over_rows(lent[0]).reshape(half_blocks, seeds, SIDE)
        theirs = products(from_away, panel, tiles, own_blocks, False)
        theirs = lax.ppermute(theirs, "col", swap)
        mine = products(from_near, panel, tiles, own_blocks, False, coded=False)
        spread = call(
            functools.partial(hub_kernel, last, own_blocks),
            score_type if last else panel_type,
            [over_chips(join(mine, theirs, late, 0 if last else LATE_JOIN)), seed_ids[None, :], out_degree],
        )
    return (spread, lent[1])


def solution(mesh):
    placed = (
        P(("row", "col"), None, None),
        P(("row", "col"), None),
        P(("row", "col")),
        P(("row", "col"), None),
        P("row"),
        P("col"),
        P(),
    )
    return jax.shard_map(
        per_device,
        mesh=mesh,
        in_specs=placed,
        out_specs=(P(("row", "col"), None), P(("col", "row"), None)),
        check_vma=False,
    )
```
